32 devices in a mesh: dp: 4 (over y, core), space: 8 (over z, x).
Axes of the slice: x: 2, y: 2, z: 4, core: 2. Of those that a mesh axis runs over, the one named last changes fastest.
Arguments:
- volume: bfloat16 [4, 4, 32, 8, 256], P('dp', None, 'space'), may hold values from -6 to 6
- first_weight: bfloat16 [27, 4, 32], replicated, may hold values from -0.875 to 0.875
- second_weight: bfloat16 [27, 32, 64], replicated, may hold values from -0.4375 to 0.4375
- third_weight: bfloat16 [27, 64, 128], replicated, may hold values from -0.3125 to 0.3125
- feature_cotangent: bfloat16 [4, 128, 4, 32], P('dp', 'space'), may hold values from -0.25 to 0.25
Outputs:
- features: bfloat16 [4, 128, 4, 32], P('dp', 'space')
- first_grad: float32 [27, 4, 32], replicated
- second_grad: float32 [27, 32, 64], replicated
- third_grad: float32 [27, 64, 128], P(None, None, 'space')
The draws below stay inside these ranges and needn't reach their ends.
All inputs are finite; a program needn't handle non-finite values.
Results may differ from the reference program's by a relative error of at most 0.0057.
Values may be sent and summed in bfloat16 or wider, within the bound.
A program may use at most 64 MiB of HBM per device.

```python
import math
import jax
import jax.numpy as jnp
from jax import lax

C0 = 4
C1 = 32
C2 = 64
C3 = 128
NX = 256
NY = 8
SAMPLES = 4
NZ = 32
Z4 = 4
YX4 = 32
N_SPACE = 8


def levels(key, shape, split, least, high):
    loudness = 1.0
    for axis_at, blocks in split:
        steps = jax.random.uniform(jax.random.fold_in(jax.random.fold_in(key, 6), axis_at), (blocks,), jnp.float32, least / len(split), high / len(split))
        loudness = loudness * jnp.repeat(jnp.exp(steps), shape[axis_at] // blocks).reshape((-1,) + (1,) * (len(shape) - 1 - axis_at))
    return loudness


def scatter_about(rng, dims, spread, most, shards=(), held_as=jnp.bfloat16):
    loudness = levels(rng, dims, shards, -0.22, 0.18) if shards else 1.0
    values = jax.random.normal(rng, dims, jnp.float32) * spread * loudness
    return jnp.minimum(jnp.maximum(values, -most), most).astype(held_as)


def setup_inputs(seed: int = 0) -> dict:
    keys = jax.random.split(jax.random.key(seed), 6)
    return {
        "volume": scatter_about(keys[0], (SAMPLES, C0, NZ, NY, NX), 1.0, 6.0, ((0, 4), (2, 8))),
        "first_weight": scatter_about(keys[1], (27, C0, C1), (27 * C0 // 2) ** -0.5, 0.875),
        "second_weight": scatter_about(keys[2], (27, C1, C2), (27 * C1 // 4) ** -0.5, 0.4375),
        "third_weight": scatter_about(keys[3], (27, C2, C3), (27 * C2 // 4) ** -0.5, 0.3125),
        "feature_cotangent": scatter_about(keys[4], (SAMPLES, C3, Z4, YX4), 0.04, 0.25, ((0, 4), (1, 8))),
    }


negative_slope = 0.3

def leaky_relu(preact):
    return negative_slope * preact + (1.0 - negative_slope) * jax.nn.softplus(preact)

def relu_slope(preact):
    return negative_slope + (1.0 - negative_slope) * jax.nn.sigmoid(preact)

def narrow_cast(values):
    return lax.optimization_barrier(values.astype(jnp.bfloat16)).astype(jnp.float32)

def pool_cells(active):
    channels, planes, height, breadth = active.shape
    blocks = active.reshape(channels, planes // 2, 2, height // 2, 2, breadth // 2, 2)
    return lax.optimization_barrier(jnp.sum(blocks, axis=(2, 4, 6))) * 0.125

def spread_cells(values):
    channels, planes, height, breadth = values.shape
    wide = jnp.broadcast_to(values[:, :, None, :, None, :, None], (channels, planes, 2, height, 2, breadth, 2))
    return wide.reshape(channels, planes * 2, height * 2, breadth * 2)

def conv_cells(field, weight, depth_pad):
    in_width, out_width = (weight.shape[1], weight.shape[2])
    kernel = weight.reshape(3, 3, 3, in_width, out_width)
    result = lax.conv_general_dilated(field[None], kernel, (1, 1, 1), ((depth_pad, depth_pad), (1, 1), (1, 1)), dimension_numbers=('NCDHW', 'DHWIO', 'NCDHW'), precision=lax.Precision.HIGHEST)
    return result[0]

def flip_weight(weight):
    in_width, out_width = (weight.shape[1], weight.shape[2])
    kernel = weight.reshape(3, 3, 3, in_width, out_width)[::-1, ::-1, ::-1].transpose(0, 1, 2, 4, 3)
    return kernel.reshape(27, out_width, in_width)

def pad_cells(field):
    return jnp.pad(field, ((0, 0), (1, 1), (1, 1), (1, 1)))

def weight_grad(padded, gradient):
    out_width, planes, height, breadth = gradient.shape
    flat_grad = gradient.reshape(out_width, planes * height * breadth)
    taps = []
    for tap_z in range(3):
        for tap_y in range(3):
            for tap_x in range(3):
                window = padded[:, tap_z:tap_z + planes, tap_y:tap_y + height, tap_x:tap_x + breadth]
                window = window.reshape(padded.shape[0], planes * height * breadth)
                taps.append(lax.dot_general(window, flat_grad, (((1,), (1,)), ((), ())), precision=lax.Precision.HIGHEST))
    return jnp.stack(taps)

def reference(volume, first_weight, second_weight, third_weight, feature_cotangent):
    kernel_one = first_weight.astype(jnp.float32)
    kernel_two = second_weight.astype(jnp.float32)
    kernel_three = third_weight.astype(jnp.float32)
    blocks = math.gcd(N_SPACE, 16)
    block_z = NZ // blocks
    block_index = jnp.arange(blocks, dtype=jnp.int32)

    def sample_pass(pair):
        volume_one, cotangent_one = pair
        depth_padded = jnp.pad(volume_one.astype(jnp.float32), ((0, 0), (1, 1), (0, 0), (0, 0)))

        def first_window(index):
            start = (index * block_z).astype(jnp.int32)
            return lax.dynamic_slice_in_dim(depth_padded, start, block_z + 2, 1)

        def first_forward(index):
            preact = conv_cells(first_window(index), kernel_one, 0)
            return narrow_cast(pool_cells(leaky_relu(preact)))
        pooled_blocks = lax.map(first_forward, block_index)
        pooled_one = jnp.moveaxis(pooled_blocks, 0, 1).reshape(C1, NZ // 2, NY // 2, NX // 2)
        preact_two = conv_cells(pooled_one, kernel_two, 1)
        pooled_two = narrow_cast(pool_cells(leaky_relu(preact_two)))
        preact_three = conv_cells(pooled_two, kernel_three, 1)
        features = pool_cells(leaky_relu(preact_three)).astype(jnp.bfloat16)
        cotangent = cotangent_one.astype(jnp.float32).reshape(C3, NZ // 8, NY // 8, NX // 8)
        grad_three = narrow_cast(spread_cells(cotangent) * 0.125 * relu_slope(preact_three))
        third = weight_grad(pad_cells(pooled_two), grad_three)
        back_two = conv_cells(grad_three, flip_weight(kernel_three), 1)
        grad_two = narrow_cast(spread_cells(back_two) * 0.125 * relu_slope(preact_two))
        second = weight_grad(pad_cells(pooled_one), grad_two)
        back_one = conv_cells(grad_two, flip_weight(kernel_two), 1)

        def first_backward(index):
            window = first_window(index)
            preact = conv_cells(window, kernel_one, 0)
            start = (index * (block_z // 2)).astype(jnp.int32)
            part = lax.dynamic_slice_in_dim(back_one, start, block_z // 2, 1)
            gradient = narrow_cast(spread_cells(part) * 0.125 * relu_slope(preact))
            padded = jnp.pad(window, ((0, 0), (0, 0), (1, 1), (1, 1)))
            return weight_grad(padded, gradient)
        first = lax.optimization_barrier(jnp.sum(lax.map(first_backward, block_index), axis=0))
        return (features.reshape(C3, NZ // 8, NY // 8 * (NX // 8)), first, second, third)
    features, first, second, third = lax.map(sample_pass, (volume, feature_cotangent))
    return (features, lax.optimization_barrier(jnp.sum(first, axis=0)), lax.optimization_barrier(jnp.sum(second, axis=0)), lax.optimization_barrier(jnp.sum(third, axis=0)))
```

```python
import functools

import jax
import jax.numpy as jnp
from jax import lax
from jax.experimental import pallas as pl
from jax.experimental.pallas import tpu as pltpu
from jax.sharding import PartitionSpec as P

MESH = pl.DeviceIdType.MESH
F32 = jnp.float32
BF16 = jnp.bfloat16
VM = pl.BlockSpec(memory_space=pltpu.VMEM)
nt = (((1,), (1,)), ((), ()))


def mm(a, b):
    return jnp.dot(a, b, preferred_element_type=F32)


def halves(v):
    hi = v.astype(BF16)
    return hi, (v - hi.astype(F32)).astype(BF16)


def mm2(v, b):
    hi, lo = halves(v)
    return mm(hi, b) + mm(lo, b)


def activate(v):
    e = jnp.exp(-jnp.abs(v))
    d = 1.0 + e
    leaky = 0.3 * v + 0.7 * (jnp.maximum(v, 0.0) + jnp.log1p(e))
    slope = 0.3 + 0.7 * (jnp.where(v >= 0.0, 1.0, e) / d)
    return leaky, slope


def shifts(x, width):
    length = x.shape[1]
    lane = lax.broadcasted_iota(jnp.int32, x.shape, 1)
    column = lane % width
    zero = jnp.zeros_like(x)
    sides = (
        jnp.where(column >= 1, pltpu.roll(x, 1, 1), zero),
        x,
        jnp.where(column < width - 1, pltpu.roll(x, length - 1, 1), zero),
    )
    taps = []
    for dy in range(3):
        for side in sides:
            if dy == 0:
                tap = jnp.where(lane >= width, pltpu.roll(side, width, 1), zero)
            elif dy == 1:
                tap = side
            else:
                tap = jnp.where(
                    lane < length - width, pltpu.roll(side, length - width, 1), zero
                )
            taps.append(tap)
    return taps


def pool_matrix(shape, width, flip=False):
    a = lax.broadcasted_iota(jnp.int32, shape, 1 if flip else 0)
    b = lax.broadcasted_iota(jnp.int32, shape, 0 if flip else 1)
    row = a // (2 * width)
    return (row * (width // 2) + (a % width) // 2 == b).astype(F32).astype(BF16)


def first_kernel(x_ref, w_ref, pooled_ref, slope_ref, taps_ref):
    taps = shifts(x_ref[...].astype(F32), 256)
    taps = jnp.concatenate(taps + [jnp.zeros((40, taps[0].shape[1]), F32)], axis=0)
    taps_ref[...] = taps.astype(BF16)
    active, slope = activate(mm(w_ref[...], taps_ref[...]))
    slope_ref[...] = slope
    deep = jnp.concatenate(
        [active[0:32] + active[32:64], active[64:96] + active[96:128]], axis=0
    )
    pool = pool_matrix((256, 128), 256)
    for y in range(4):
        low = deep[:, y * 512 : y * 512 + 256]
        high = deep[:, y * 512 + 256 : y * 512 + 512]
        pooled_ref[:, y * 128 : y * 128 + 128] = (mm2(low + high, pool) * 0.125).astype(BF16)


def second_kernel(x_ref, w_ref, pooled_ref, slope_ref, taps_ref):
    taps = jnp.concatenate(shifts(x_ref[...].astype(F32), 128), axis=0)
    taps_ref[...] = taps.astype(BF16)
    active, slope = activate(mm(w_ref[...], taps_ref[...]))
    slope_ref[...] = slope
    deep = active[0:64] + active[64:128]
    pool = pool_matrix((512, 128), 128)
    pooled_ref[...] = (mm2(deep, pool) * 0.125).astype(BF16)


def third_kernel(x_ref, w_ref, c_ref, grad_ref, paired_ref, weight_ref):
    taps = jnp.concatenate(shifts(x_ref[...].astype(F32), 64), axis=0).astype(BF16)
    active, slope = activate(mm(w_ref[...], taps))
    paired_ref[...] = mm2(active, pool_matrix((128, 32), 64))
    wide = mm(c_ref[...], pool_matrix((32, 128), 64, True))
    grad = (wide * 0.125 * slope).astype(BF16)
    grad_ref[...] = grad
    taps = jnp.concatenate([taps, jnp.zeros((320, 128), BF16)], axis=0)
    for part in range(4):
        piece = taps[part * 512 : part * 512 + 512]
        weight_ref[part] = lax.dot_general(
            grad, piece, nt, preferred_element_type=F32
        ).astype(BF16)


def fourth_kernel(g_ref, w_ref, slope_ref, taps_ref, grad_ref, weight_ref):
    taps = jnp.concatenate(shifts(g_ref[...].astype(F32), 64), axis=0).astype(BF16)
    back = mm(w_ref[...], taps)
    wide = mm2(back, pool_matrix((128, 512), 128, True)) * 0.125
    grad = (jnp.concatenate([wide, wide], axis=0) * slope_ref[...]).astype(BF16)
    grad_ref[...] = grad
    total = lax.dot_general(grad, taps_ref[...], nt, preferred_element_type=F32)
    total = total[0:64] + pltpu.roll(total[64:128], total.shape[1] - 32, 1)
    for k in range(9):
        weight_ref[k * 64 : k * 64 + 64, :] = total[:, k * 128 : k * 128 + 128]


def fifth_kernel(g_ref, w_ref, slope_ref, taps_ref, weight_ref, grad_ref, wide_ref):
    wide_ref[...] = jnp.concatenate(shifts(g_ref[...].astype(F32), 128), axis=0).astype(BF16)
    back = mm(w_ref[...], wide_ref[...])
    pool = pool_matrix((128, 256), 256, True)
    for y in range(4):
        wide = mm2(back[:, y * 128 : y * 128 + 128], pool) * 0.125
        wide = jnp.concatenate([wide[0:32], wide[0:32], wide[32:64], wide[32:64]], axis=0)
        for part in range(2):
            at = y * 512 + part * 256
            grad_ref[:, at : at + 256] = (wide * slope_ref[:, at : at + 256]).astype(BF16)
    total = lax.dot_general(grad_ref[...], taps_ref[...], nt, preferred_element_type=F32)
    result = total[0:32]
    for z in range(1, 4):
        result = result + pltpu.roll(total[32 * z : 32 * z + 32], 256 - 4 * z, 1)
    weight_ref[...] = jnp.concatenate([result[:, 0:128], result[:, 128:256]], axis=0)


def call(kernel, outs, scratch=()):
    return pl.pallas_call(
        kernel,
        out_shape=[jax.ShapeDtypeStruct(s, d) for s, d in outs],
        out_specs=[VM] * len(outs),
        scratch_shapes=list(scratch),
        compiler_params=pltpu.CompilerParams(vmem_limit_bytes=48 << 20),
    )


def greet(axes):
    barrier = pltpu.get_barrier_semaphore()
    count = 0
    for axis, n in axes:
        me = lax.axis_index(axis)
        for k in range(1, n):
            pl.semaphore_signal(
                barrier, inc=1, device_id={axis: lax.rem(me + k, n)}, device_id_type=MESH
            )
            count += 1
    pl.semaphore_wait(barrier, count)


def spread_to(axis, n, send, recv, source, target):
    me = lax.axis_index(axis)
    copies = []
    for k in range(1, n):
        peer = lax.rem(me + k, n)
        copy = pltpu.make_async_remote_copy(
            src_ref=source(peer),
            dst_ref=target(k),
            send_sem=send.at[k],
            recv_sem=recv.at[k],
            device_id={axis: peer},
            device_id_type=MESH,
        )
        copy.start()
        copies.append(copy)
    return copies


def finish(copies):
    for copy in copies:
        copy.wait()


def reduce_kernel(
    nd, n, a_ref, b_ref, p_ref, a_out, b_out, p_out,
    a_slot, b_slot, a_sum, b_sum, a_next, b_next, b_mid, sends, recvs,
):
    d = lax.axis_index("dp")
    s = lax.axis_index("space")
    greet((("dp", nd), ("space", n)))
    one = spread_to("dp", nd, sends.at[0], recvs.at[0], lambda p: a_ref.at[p], lambda k: a_slot.at[k])
    two = spread_to("dp", nd, sends.at[1], recvs.at[1], lambda p: b_ref.at[p], lambda k: b_slot.at[k])
    six = spread_to("space", n, sends.at[2], recvs.at[2], lambda p: p_ref.at[p], lambda k: p_out.at[s])
    p_out[s] = p_ref[s]
    finish(two)
    total = b_ref[d]
    for k in range(1, nd):
        total = total + b_slot[k]
    b_sum[...] = total
    three = spread_to("space", n, sends.at[3], recvs.at[3], lambda p: b_sum.at[p], lambda k: b_next.at[k])
    finish(one)
    total = a_ref[d].astype(F32)
    for k in range(1, nd):
        total = total + a_slot[k].astype(F32)
    a_sum[...] = total
    four = spread_to("space", n, sends.at[4], recvs.at[4], lambda p: a_sum.at[p], lambda k: a_next.at[k])
    finish(three)
    total = b_sum[s]
    for k in range(1, n):
        total = total + b_next[k]
    b_mid[d] = total
    three = spread_to("dp", nd, sends.at[5], recvs.at[5], lambda p: b_mid.at[d], lambda k: b_mid.at[d])
    finish(three)
    b_out[s] = b_mid[...]
    three = spread_to("space", n, sends.at[6], recvs.at[6], lambda p: b_mid, lambda k: b_out.at[s])
    finish(four)
    total = a_sum[s]
    for k in range(1, n):
        total = total + a_next[k]
    a_out[d] = total
    four = spread_to("dp", nd, sends.at[7], recvs.at[7], lambda p: a_out.at[d], lambda k: a_out.at[d])
    finish(four)
    finish(three)
    finish(six)


def reduce_all(nd, n, a, b, p):
    share = a.shape[2]
    rows = b.shape[2]
    most = max(nd, n)
    return pl.pallas_call(
        functools.partial(reduce_kernel, nd, n),
        out_shape=[
            jax.ShapeDtypeStruct((nd, share, 512), F32),
            jax.ShapeDtypeStruct((n, nd, rows, 128), F32),
            jax.ShapeDtypeStruct(p.shape, F32),
        ],
        in_specs=[VM] * 3,
        out_specs=[VM] * 3,
        scratch_shapes=[
            pltpu.VMEM((nd, n, share, 512), BF16),
            pltpu.VMEM((nd, n, rows, 128), F32),
            pltpu.VMEM((n, share, 512), F32),
            pltpu.VMEM((n, rows, 128), F32),
            pltpu.VMEM((n, share, 512), F32),
            pltpu.VMEM((n, rows, 128), F32),
            pltpu.VMEM((nd, rows, 128), F32),
            pltpu.SemaphoreType.DMA((8, most)),
            pltpu.SemaphoreType.DMA((8, most)),
        ],
        compiler_params=pltpu.CompilerParams(
            collective_id=1, has_side_effects=True, vmem_limit_bytes=48 << 20
        ),
    )(a, b, p)


def banded(weight, planes):
    taps, in_width, out_width = weight.shape
    kernel = weight.reshape(3, 9, in_width, out_width).transpose(3, 1, 0, 2)
    rows = [
        jnp.pad(kernel, ((0, 0), (0, 0), (z, planes - 1 - z), (0, 0))) for z in range(planes)
    ]
    return jnp.stack(rows).reshape(planes * out_width, 9 * (planes + 2) * in_width)


def mirrored(weight):
    return weight[::-1].transpose(0, 2, 1)


def rim(block, n, width):
    forward = [(i, i + 1) for i in range(n - 1)]
    backward = [(target, source) for source, target in forward]
    low = lax.ppermute(block[-width:], "space", forward)
    high = lax.ppermute(block[:width], "space", backward)
    return jnp.concatenate([low, block, high], axis=0)


def body(nd, n, volume, first_weight, second_weight, third_weight, feature_cotangent):
    share = feature_cotangent.shape[1]
    depth = feature_cotangent.shape[2]
    planes = volume[0].transpose(1, 0, 2, 3).reshape(16, 2048)
    weight_one = jnp.pad(banded(first_weight, 4), ((0, 0), (0, 40)))
    weight_two = banded(second_weight, 2)
    weight_three = banded(third_weight, 1)
    flip_three = banded(mirrored(third_weight), 1)
    flip_two = banded(mirrored(second_weight), 2)
    spread = jnp.repeat(feature_cotangent[0], 2, axis=1)
    cotangent = lax.all_to_all(spread, "space", split_axis=1, concat_axis=0, tiled=True)
    cotangent = cotangent.reshape(128, 32)

    pooled_one, slope_one, taps_one = call(
        first_kernel, [((64, 512), BF16), ((128, 2048), F32), ((256, 2048), BF16)]
    )(rim(planes, n, 4), weight_one)
    pooled_two, slope_two, taps_two = call(
        second_kernel, [((64, 128), BF16), ((128, 512), F32), ((1152, 512), BF16)]
    )(rim(pooled_one, n, 32), weight_two)
    grad_three, paired, part_three = call(
        third_kernel, [((128, 128), BF16), ((128, 32), F32), ((4, 128, 512), BF16)]
    )(rim(pooled_two, n, 64), weight_three, cotangent)
    grad_two, part_two = call(
        fourth_kernel, [((128, 512), BF16), ((576, 128), F32)]
    )(rim(grad_three, n, 128), flip_three, slope_two, taps_two)
    (part_one,) = call(
        fifth_kernel,
        [((64, 128), F32)],
        [pltpu.VMEM((128, 2048), BF16), pltpu.VMEM((2304, 512), BF16)],
    )(rim(grad_two, n, 64), flip_two, slope_one, taps_one)

    parts = jnp.concatenate([part_two, part_one, jnp.zeros((384, 128), F32)], axis=0)
    third, rest, turned = reduce_all(
        nd,
        n,
        part_three.reshape(nd, n, share, 2048 // nd),
        parts.reshape(nd, n, 1024 // (nd * n), 128),
        paired.reshape(n, share, 32),
    )
    features = turned.reshape(depth, 2, share, 32).sum(axis=1) * 0.125
    features = features.transpose(1, 0, 2).astype(BF16)[None]
    third = third.transpose(1, 0, 2).reshape(share, 2048)[:, :1728]
    third_grad = third.reshape(share, 9, 3, 64).transpose(2, 1, 3, 0).reshape(27, 64, share)
    rest = rest.transpose(1, 0, 2, 3).reshape(1024, 128)
    second = rest[:576].reshape(9, 64, 4, 32)[:, :, :3]
    second_grad = second.transpose(2, 0, 3, 1).reshape(27, 32, 64)
    first = rest[576:640].reshape(2, 32, 128).transpose(1, 0, 2).reshape(32, 256)
    first = first[:, :216].reshape(32, 9, 6, 4)[:, :, :3]
    first_grad = first.transpose(2, 1, 3, 0).reshape(27, 4, 32)
    return (features, first_grad, second_grad, third_grad)


def solution(mesh):
    return jax.shard_map(
        functools.partial(body, mesh.shape["dp"], mesh.shape["space"]),
        mesh=mesh,
        in_specs=(P("dp", None, "space", None, None), P(), P(), P(), P("dp", "space", None, None)),
        out_specs=(P("dp", "space", None, None), P(), P(), P(None, None, "space")),
        check_vma=False,
    )
```

```python
import functools

import jax
import jax.numpy as jnp
from jax import lax
from jax.experimental import pallas as pl
from jax.experimental.pallas import tpu as pltpu
from jax.sharding import PartitionSpec as P

MESH = pl.DeviceIdType.MESH
F32 = jnp.float32
BF16 = jnp.bfloat16
VM = pl.BlockSpec(memory_space=pltpu.VMEM)
nt = (((1,), (1,)), ((), ()))


def mm(a, b):
    return jnp.dot(a, b, preferred_element_type=F32)


def halves(v):
    hi = v.astype(BF16)
    return hi, (v - hi.astype(F32)).astype(BF16)


def mm2(v, b):
    hi, lo = halves(v)
    return mm(hi, b) + mm(lo, b)


def activate(v):
    e = jnp.exp(-jnp.abs(v))
    d = 1.0 + e
    leaky = 0.3 * v + 0.7 * (jnp.maximum(v, 0.0) + jnp.log1p(e))
    slope = 0.3 + 0.7 * (jnp.where(v >= 0.0, 1.0, e) / d)
    return leaky, slope


def shifts(x, width):
    length = x.shape[1]
    lane = lax.broadcasted_iota(jnp.int32, x.shape, 1)
    column = lane % width
    zero = jnp.zeros_like(x)
    sides = (
        jnp.where(column >= 1, pltpu.roll(x, 1, 1), zero),
        x,
        jnp.where(column < width - 1, pltpu.roll(x, length - 1, 1), zero),
    )
    taps = []
    for dy in range(3):
        for side in sides:
            if dy == 0:
                tap = jnp.where(lane >= width, pltpu.roll(side, width, 1), zero)
            elif dy == 1:
                tap = side
            else:
                tap = jnp.where(
                    lane < length - width, pltpu.roll(side, length - width, 1), zero
                )
            taps.append(tap)
    return taps


def pool_matrix(shape, width, flip=False):
    a = lax.broadcasted_iota(jnp.int32, shape, 1 if flip else 0)
    b = lax.broadcasted_iota(jnp.int32, shape, 0 if flip else 1)
    row = a // (2 * width)
    return (row * (width // 2) + (a % width) // 2 == b).astype(F32).astype(BF16)


def tn(a, b):
    return lax.dot_general(a, b, (((0,), (0,)), ((), ())), preferred_element_type=F32)


def mnt(a, b):
    return lax.dot_general(a, b, nt, preferred_element_type=F32)


def greet(axes):
    barrier = pltpu.get_barrier_semaphore()
    count = 0
    for axis, n in axes:
        me = lax.axis_index(axis)
        for k in range(1, n):
            pl.semaphore_signal(
                barrier, inc=1, device_id={axis: lax.rem(me + k, n)}, device_id_type=MESH
            )
            count += 1
    pl.semaphore_wait(barrier, count)


def spread_to(axis, n, send, recv, source, target):
    me = lax.axis_index(axis)
    copies = []
    for k in range(1, n):
        peer = lax.rem(me + k, n)
        copy = pltpu.make_async_remote_copy(
            src_ref=source(peer),
            dst_ref=target,
            send_sem=send.at[k],
            recv_sem=recv.at[k],
            device_id={axis: peer},
            device_id_type=MESH,
        )
        copy.start()
        copies.append(copy)
    return copies


def finish(copies):
    for copy in copies:
        copy.wait()


def added(slots, count):
    total = slots[0].astype(F32)
    for k in range(1, count):
        total = total + slots[k].astype(F32)
    return total


class Halo:
    def __init__(self, n, send, recv, first, last, low, high):
        s = lax.axis_index("space")
        self.has_low, self.has_high = s > 0, s < n - 1
        self.up = pltpu.make_async_remote_copy(
            src_ref=last, dst_ref=low, send_sem=send.at[0], recv_sem=recv.at[0],
            device_id={"space": lax.rem(s + 1, n)}, device_id_type=MESH,
        )
        self.down = pltpu.make_async_remote_copy(
            src_ref=first, dst_ref=high, send_sem=send.at[1], recv_sem=recv.at[1],
            device_id={"space": lax.rem(s + n - 1, n)}, device_id_type=MESH,
        )

        @pl.when(self.has_high)
        def _():
            self.up.start()

        @pl.when(self.has_low)
        def _():
            self.down.start()

        @pl.when(s == 0)
        def _():
            low[...] = jnp.zeros_like(low)

        @pl.when(s == n - 1)
        def _():
            high[...] = jnp.zeros_like(high)

    def wait(self):
        @pl.when(self.has_high)
        def _():
            self.down.wait_recv()

        @pl.when(self.has_low)
        def _():
            self.up.wait_recv()

        @pl.when(self.has_high)
        def _():
            self.up.wait_send()

        @pl.when(self.has_low)
        def _():
            self.down.wait_send()


def lay_taps(into, at, block, width):
    taps = jnp.concatenate(shifts(block.astype(F32), width), axis=0).astype(BF16)
    into[at : at + taps.shape[0], :] = taps


def step_kernel(
    nd, n, share, volume, weight_one, weight_two, weight_three, cotangent,
    a_out, b_out, c_out, p_out,
    rim_zero, rim_one, rim_two, rim_three, rim_four, cot_all,
    taps_one, taps_two, taps_three, wide_three, wide_two, slope_one, grad_one, back_two,
    p_src, a_src, a_slot, a_sum, a_next, b_src, b_slot, b_sum, b_next, b_mid,
    c_src, c_slot, c_sum, c_next, halo_send, halo_recv, sends, recvs,
):
    d = lax.axis_index("dp")
    s = lax.axis_index("space")
    greet((("dp", nd), ("space", n)))

    def halo(index, first, last, low, high):
        return Halo(n, halo_send.at[index], halo_recv.at[index], first, last, low, high)

    def spread(index, axis, source, target):
        return spread_to(
            axis, nd if axis == "dp" else n, sends.at[index], recvs.at[index], source, target
        )

    edge = halo(0, volume.at[0], volume.at[3], rim_zero.at[0], rim_zero.at[1])
    cot_all[s] = cotangent[lax.div(s, 2)]
    cots = spread(0, "space", lambda p: cotangent.at[lax.div(p, 2)], cot_all.at[s])
    for t in range(27):
        back_two[:, t * 64 : t * 64 + 64] = weight_two[26 - t]
    taps_two[1152:1184, :] = jnp.zeros((32, 512), BF16)
    taps_three[1728:2048, :] = jnp.zeros((320, 128), BF16)
    edge.wait()

    planes = [rim_zero[0]] + [volume[z] for z in range(4)] + [rim_zero[1]]
    planes = jnp.concatenate([plane.astype(F32) for plane in planes], axis=0)
    taps = shifts(planes, 256)
    taps = jnp.concatenate(taps + [jnp.zeros((40, 2048), F32)], axis=0)
    taps_one[...] = taps.astype(BF16)
    active, slope = activate(mm(weight_one[...], taps_one[...]))
    slope_one[...] = slope
    deep = jnp.concatenate(
        [active[0:32] + active[32:64], active[64:96] + active[96:128]], axis=0
    )
    pool = pool_matrix((256, 128), 256)
    for y in range(4):
        low = deep[:, y * 512 : y * 512 + 256]
        high = deep[:, y * 512 + 256 : y * 512 + 512]
        pooled = (mm2(low + high, pool) * 0.125).astype(BF16)
        rim_one[1, :, y * 128 : y * 128 + 128] = pooled[0:32]
        rim_one[2, :, y * 128 : y * 128 + 128] = pooled[32:64]

    edge = halo(1, rim_one.at[1], rim_one.at[2], rim_one.at[0], rim_one.at[3])
    for z in (1, 2):
        lay_taps(taps_two, z * 288, rim_one[z], 128)
    edge.wait()
    for z in (0, 3):
        lay_taps(taps_two, z * 288, rim_one[z], 128)
    kernel_two = weight_two[...].reshape(864, 64)
    pairs = [activate(tn(kernel_two, taps_two[z * 288 : z * 288 + 864, :])) for z in range(2)]
    slope_two = [pair[1] for pair in pairs]
    pool = pool_matrix((512, 128), 128)
    rim_two[1] = (mm2(pairs[0][0] + pairs[1][0], pool) * 0.125).astype(BF16)

    edge = halo(2, rim_two.at[1], rim_two.at[1], rim_two.at[0], rim_two.at[2])
    lay_taps(taps_three, 576, rim_two[1], 64)
    finish(cots)
    cot = jnp.concatenate([cot_all[i] for i in range(n)], axis=0).astype(BF16)
    wide = mm(cot, pool_matrix((32, 128), 64, True)) * 0.125
    edge.wait()
    for z in (0, 2):
        lay_taps(taps_three, z * 576, rim_two[z], 64)
    kernel_three = weight_three[...].reshape(1728, 128)
    active, slope = activate(tn(kernel_three, taps_three[0:1728, :]))
    grad = (wide * slope).astype(BF16)
    rim_three[1] = grad

    edge = halo(3, rim_three.at[1], rim_three.at[1], rim_three.at[0], rim_three.at[2])
    lay_taps(wide_three, 1152, grad, 64)
    for part in range(4):
        term = mnt(grad, taps_three[part * 512 : part * 512 + 512, :])
        for i in range(n):
            a_src[part, i] = term[i * share : i * share + share].astype(BF16)
    a_slot[d] = a_src[d]
    a_first = spread(1, "dp", lambda p: a_src.at[p], a_slot.at[d])
    paired = mm2(active, pool_matrix((128, 32), 64))
    for i in range(n):
        p_src[i] = paired[i * share : i * share + share]
    p_out[s] = p_src[s]
    feats = spread(2, "space", lambda p: p_src.at[p], p_out.at[s])
    edge.wait()
    for z in (0, 2):
        lay_taps(wide_three, z * 1152, rim_three[z], 64)
    flipped = jnp.concatenate([weight_three[26 - t] for t in range(27)], axis=1)
    back = mm(flipped, wide_three[...])
    wide = mm2(back, pool_matrix((128, 512), 128, True)) * 0.125
    grads = [(wide * slope_two[z]).astype(BF16) for z in range(2)]
    for z in range(2):
        rim_four[z + 1] = grads[z]

    edge = halo(4, rim_four.at[1], rim_four.at[2], rim_four.at[0], rim_four.at[3])
    total = mnt(grads[0], taps_two[0:896, :]) + mnt(grads[1], taps_two[288:1184, :])
    stack = jnp.concatenate([total[:, k * 128 : k * 128 + 128] for k in range(7)], axis=0)
    rows = b_src.shape[2]
    for i in range(nd * n):
        piece = stack[i * rows : i * rows + rows]
        if piece.shape[0] < rows:
            piece = jnp.zeros((rows, 128), F32)
        b_src[i // n, i % n] = piece
    b_slot[d] = b_src[d]
    b_first = spread(3, "dp", lambda p: b_src.at[p], b_slot.at[d])
    for z in (1, 2):
        lay_taps(wide_two, z * 576, rim_four[z], 128)
    finish(a_first)
    a_sum[...] = added(a_slot, nd)
    a_next[s] = a_sum[s]
    a_second = spread(4, "space", lambda p: a_sum.at[p], a_next.at[s])
    edge.wait()
    for z in (0, 3):
        lay_taps(wide_two, z * 576, rim_four[z], 128)
    backs = [mm(back_two[...], wide_two[z * 576 : z * 576 + 1728, :]) for z in range(2)]
    pool = pool_matrix((128, 256), 256, True)
    for y in range(4):
        wides = [mm2(back[:, y * 128 : y * 128 + 128], pool) * 0.125 for back in backs]
        wide = jnp.concatenate([wides[0], wides[0], wides[1], wides[1]], axis=0)
        for part in range(2):
            at = y * 512 + part * 256
            grad_one[:, at : at + 256] = (wide * slope_one[:, at : at + 256]).astype(BF16)
    total = mnt(grad_one[...], taps_one[...])
    result = total[0:32]
    for z in range(1, 4):
        result = result + pltpu.roll(total[32 * z : 32 * z + 32], 256 - 4 * z, 1)
    c_src[...] = jnp.concatenate([result[:, 0:128], result[:, 128:256]], axis=0)
    c_slot[d] = c_src[...]
    c_first = spread(5, "dp", lambda p: c_src, c_slot.at[d])

    finish(b_first)
    b_sum[...] = added(b_slot, nd)
    b_next[s] = b_sum[s]
    b_second = spread(6, "space", lambda p: b_sum.at[p], b_next.at[s])
    finish(c_first)
    total = added(c_slot, nd)
    rows = c_sum.shape[1]
    for i in range(n):
        piece = total[i * rows : i * rows + rows]
        if piece.shape[0] < rows:
            piece = jnp.zeros((rows, 128), F32)
        c_sum[i] = piece
    c_next[s] = c_sum[s]
    c_second = spread(7, "space", lambda p: c_sum.at[p], c_next.at[s])
    finish(a_second)
    a_out[d] = added(a_next, n)
    a_third = spread(8, "dp", lambda p: a_out.at[d], a_out.at[d])
    finish(b_second)
    b_mid[d] = added(b_next, n)
    b_third = spread(9, "dp", lambda p: b_mid.at[d], b_mid.at[d])
    finish(c_second)
    c_out[s] = added(c_next, n)
    c_third = spread(10, "space", lambda p: c_out.at[s], c_out.at[s])
    finish(b_third)
    b_out[s] = b_mid[...]
    b_last = spread(11, "space", lambda p: b_mid, b_out.at[s])
    for copies in (feats, a_third, c_third, b_last):
        finish(copies)


def banded(weight, planes):
    taps, in_width, out_width = weight.shape
    kernel = weight.reshape(3, 9, in_width, out_width).transpose(3, 1, 0, 2)
    rows = [
        jnp.pad(kernel, ((0, 0), (0, 0), (z, planes - 1 - z), (0, 0))) for z in range(planes)
    ]
    return jnp.stack(rows).reshape(planes * out_width, 9 * (planes + 2) * in_width)


def body(nd, n, volume, first_weight, second_weight, third_weight, feature_cotangent):
    share = feature_cotangent.shape[1]
    depth = feature_cotangent.shape[2]
    planes = volume[0].transpose(1, 0, 2, 3).reshape(4, 4, 2048)
    weight_one = jnp.pad(banded(first_weight, 4), ((0, 0), (0, 40)))
    cotangent = feature_cotangent[0].transpose(1, 0, 2).astype(F32)
    b_rows = pl.cdiv(448, nd * n)
    c_rows = pl.cdiv(64, n)
    most = max(nd, n)
    scratch = [
        ((2, 4, 2048), BF16), ((4, 32, 512), BF16), ((3, 64, 128), BF16), ((3, 128, 128), BF16),
        ((4, 64, 512), BF16), ((n, share, 32), F32),
        ((256, 2048), BF16), ((1184, 512), BF16), ((2048, 128), BF16), ((3456, 128), BF16),
        ((2304, 512), BF16), ((128, 2048), F32), ((128, 2048), BF16), ((32, 1728), BF16),
        ((n, share, 32), F32), ((nd, n, share, 512), BF16), ((nd, n, share, 512), BF16),
        ((n, share, 512), F32), ((n, share, 512), F32),
        ((nd, n, b_rows, 128), F32), ((nd, n, b_rows, 128), F32), ((n, b_rows, 128), F32),
        ((n, b_rows, 128), F32), ((nd, b_rows, 128), F32),
        ((64, 128), F32), ((nd, 64, 128), F32), ((n, c_rows, 128), F32), ((n, c_rows, 128), F32),
    ]
    third, rest, first, turned = pl.pallas_call(
        functools.partial(step_kernel, nd, n, share),
        out_shape=[
            jax.ShapeDtypeStruct((nd, share, 512), F32),
            jax.ShapeDtypeStruct((n, nd, b_rows, 128), F32),
            jax.ShapeDtypeStruct((n, c_rows, 128), F32),
            jax.ShapeDtypeStruct((n, share, 32), F32),
        ],
        in_specs=[VM] * 5,
        out_specs=[VM] * 4,
        scratch_shapes=[pltpu.VMEM(shape, kind) for shape, kind in scratch]
        + [pltpu.SemaphoreType.DMA((5, 2))] * 2
        + [pltpu.SemaphoreType.DMA((12, most))] * 2,
        compiler_params=pltpu.CompilerParams(
            collective_id=1, has_side_effects=True, vmem_limit_bytes=56 << 20
        ),
    )(planes, weight_one, second_weight, third_weight, cotangent)

    features = turned.reshape(depth, 2, share, 32).sum(axis=1) * 0.125
    features = features.transpose(1, 0, 2).astype(BF16)[None]
    third = third.transpose(1, 0, 2).reshape(share, 2048)[:, :1728]
    third_grad = third.reshape(share, 27, 64).transpose(1, 2, 0)
    rest = rest.transpose(1, 0, 2, 3).reshape(nd * n * b_rows, 128)[:448]
    second = rest.reshape(7, 64, 128).transpose(1, 0, 2).reshape(64, 896)[:, :864]
    second_grad = second.T.reshape(27, 32, 64)
    first = first.reshape(n * c_rows, 128)[:64]
    first = first.reshape(2, 32, 128).transpose(1, 0, 2).reshape(32, 256)
    first = first[:, :216].reshape(32, 9, 6, 4)[:, :, :3]
    first_grad = first.transpose(2, 1, 3, 0).reshape(27, 4, 32)
    return (features, first_grad, second_grad, third_grad)


def solution(mesh):
    return jax.shard_map(
        functools.partial(body, mesh.shape["dp"], mesh.shape["space"]),
        mesh=mesh,
        in_specs=(P("dp", None, "space", None, None), P(), P(), P(), P("dp", "space", None, None)),
        out_specs=(P("dp", "space", None, None), P(), P(), P(None, None, "space")),
        check_vma=False,
    )
```

```python
import functools

import jax
import jax.numpy as jnp
import numpy as np
from jax import lax
from jax.experimental import pallas as pl
from jax.experimental.pallas import tpu as pltpu
from jax.sharding import PartitionSpec as P

MESH = pl.DeviceIdType.MESH
F32 = jnp.float32
BF16 = jnp.bfloat16
VM = pl.BlockSpec(memory_space=pltpu.VMEM)
nt = (((1,), (1,)), ((), ()))


def mm(a, b):
    return jnp.dot(a, b, preferred_element_type=F32)


def halves(v):
    hi = v.astype(BF16)
    return hi, (v - hi.astype(F32)).astype(BF16)


def mm2(v, b):
    hi, lo = halves(v)
    return mm(hi, b) + mm(lo, b)


def activate(v):
    e = jnp.exp(-jnp.abs(v))
    d = 1.0 + e
    leaky = 0.3 * v + 0.7 * (jnp.maximum(v, 0.0) + jnp.log1p(e))
    slope = 0.3 + 0.7 * (jnp.where(v >= 0.0, 1.0, e) / d)
    return leaky, slope


def shifts(x, width):
    length = x.shape[1]
    lane = lax.broadcasted_iota(jnp.int32, x.shape, 1)
    column = lane % width
    zero = jnp.zeros_like(x)
    sides = (
        jnp.where(column >= 1, pltpu.roll(x, 1, 1), zero),
        x,
        jnp.where(column < width - 1, pltpu.roll(x, length - 1, 1), zero),
    )
    taps = []
    for dy in range(3):
        for side in sides:
            if dy == 0:
                tap = jnp.where(lane >= width, pltpu.roll(side, width, 1), zero)
            elif dy == 1:
                tap = side
            else:
                tap = jnp.where(
                    lane < length - width, pltpu.roll(side, length - width, 1), zero
                )
            taps.append(tap)
    return taps


def pool_matrix(shape, width, flip=False):
    a = lax.broadcasted_iota(jnp.int32, shape, 1 if flip else 0)
    b = lax.broadcasted_iota(jnp.int32, shape, 0 if flip else 1)
    row = a // (2 * width)
    return (row * (width // 2) + (a % width) // 2 == b).astype(F32).astype(BF16)


def tn(a, b):
    return lax.dot_general(a, b, (((0,), (0,)), ((), ())), preferred_element_type=F32)


def mnt(a, b):
    return lax.dot_general(a, b, nt, preferred_element_type=F32)


def greet(axes):
    barrier = pltpu.get_barrier_semaphore()
    count = 0
    for axis, n in axes:
        me = lax.axis_index(axis)
        for k in range(1, n):
            pl.semaphore_signal(
                barrier, inc=1, device_id={axis: lax.rem(me + k, n)}, device_id_type=MESH
            )
            count += 1
    pl.semaphore_wait(barrier, count)


def spread_to(axis, n, send, recv, source, target):
    me = lax.axis_index(axis)
    copies = []
    for k in range(1, n):
        peer = lax.rem(me + k, n)
        copy = pltpu.make_async_remote_copy(
            src_ref=source(peer),
            dst_ref=target,
            send_sem=send.at[k],
            recv_sem=recv.at[k],
            device_id={axis: peer},
            device_id_type=MESH,
        )
        copy.start()
        copies.append(copy)
    return copies


def finish(copies):
    for copy in copies:
        copy.wait()


def added(slots, count):
    total = slots[0].astype(F32)
    for k in range(1, count):
        total = total + slots[k].astype(F32)
    return total


class Halo:
    def __init__(self, n, send, recv, first, last, low, high):
        s = lax.axis_index("space")
        self.has_low, self.has_high = s > 0, s < n - 1
        self.up = pltpu.make_async_remote_copy(
            src_ref=last, dst_ref=low, send_sem=send.at[0], recv_sem=recv.at[0],
            device_id={"space": lax.rem(s + 1, n)}, device_id_type=MESH,
        )
        self.down = pltpu.make_async_remote_copy(
            src_ref=first, dst_ref=high, send_sem=send.at[1], recv_sem=recv.at[1],
            device_id={"space": lax.rem(s + n - 1, n)}, device_id_type=MESH,
        )

        @pl.when(self.has_high)
        def _():
            self.up.start()

        @pl.when(self.has_low)
        def _():
            self.down.start()

        @pl.when(s == 0)
        def _():
            low[...] = jnp.zeros_like(low)

        @pl.when(s == n - 1)
        def _():
            high[...] = jnp.zeros_like(high)

    def wait(self):
        @pl.when(self.has_high)
        def _():
            self.down.wait_recv()

        @pl.when(self.has_low)
        def _():
            self.up.wait_recv()

        @pl.when(self.has_high)
        def _():
            self.up.wait_send()

        @pl.when(self.has_low)
        def _():
            self.down.wait_send()


def lay_taps(into, at, block, width):
    taps = jnp.concatenate(shifts(block.astype(F32), width), axis=0).astype(BF16)
    into[at : at + taps.shape[0], :] = taps


def step_kernel(
    nd, n, share, volume, weight_one, select, weight_two, weight_three, cotangent_in,
    a_out, b_out, c_out, p_out,
    rim_zero, rim_one, rim_two, rim_three, rim_four, cot_all,
    taps_one, taps_two, taps_three, wide_three, wide_two, slope_one, grad_one, back_two,
    p_src, a_src, a_got, a_half, a_other, a_sum, a_next, b_src, b_got, b_half, b_other, b_sum, b_next,
    c_src, c_slot, c_sum, c_next, cotangent, inner, outer, halo_send, halo_recv, sends, recvs,
):
    d = lax.axis_index("dp")
    s = lax.axis_index("space")
    greet((("dp", nd), ("space", n)))

    def halo(index, first, last, low, high):
        return Halo(n, halo_send.at[index], halo_recv.at[index], first, last, low, high)

    def spread(index, axis, source, target):
        return spread_to(
            axis, nd if axis == "dp" else n, sends.at[index], recvs.at[index], source, target
        )

    core = lax.rem(d, 2)
    row = lax.div(d, 2)
    beside = d + 1 - 2 * core
    across = lax.rem(d + 2, 4)

    def pass_to(index, slot, peer, source, target):
        copy = pltpu.make_async_remote_copy(
            src_ref=source, dst_ref=target, send_sem=sends.at[index, slot],
            recv_sem=recvs.at[index, slot], device_id={"dp": peer}, device_id_type=MESH,
        )
        copy.start()
        return copy

    edge = halo(0, volume.at[:, 0], volume.at[:, 3], rim_zero.at[0], rim_zero.at[1])
    spots = cotangent_in[...].astype(F32)
    for z in range(spots.shape[1]):
        cotangent[z] = spots[:, z, :]
    cot_all[s] = cotangent[lax.div(s, 2)]
    cots = spread(0, "space", lambda p: cotangent.at[lax.div(p, 2)], cot_all.at[s])
    for t in range(27):
        back_two[:, t * 64 : t * 64 + 64] = weight_two[26 - t]
    taps_two[1152:1184, :] = jnp.zeros((32, 512), BF16)
    taps_three[1728:2048, :] = jnp.zeros((320, 128), BF16)
    inner[...] = volume[...].astype(F32).reshape(16, 8, 256)
    band = jnp.concatenate(
        [mnt(weight_one[...], select[z * 256 : z * 256 + 256, :]) for z in range(4)], axis=0
    ).astype(BF16)
    edge.wait()

    outer[...] = rim_zero[...].astype(F32).reshape(8, 8, 256)
    planes = jnp.concatenate(
        [jnp.concatenate([inner[:, y, :], outer[:, y, :]], axis=0) for y in range(8)], axis=1
    )
    taps = shifts(planes, 256)
    taps = jnp.concatenate(taps + [jnp.zeros((40, 2048), F32)], axis=0)
    taps_one[...] = taps.astype(BF16)
    active, slope = activate(mm(band, taps_one[...]))
    slope_one[...] = slope
    deep = jnp.concatenate(
        [active[0:32] + active[32:64], active[64:96] + active[96:128]], axis=0
    )
    pool = pool_matrix((256, 128), 256)
    for y in range(4):
        low = deep[:, y * 512 : y * 512 + 256]
        high = deep[:, y * 512 + 256 : y * 512 + 512]
        pooled = (mm2(low + high, pool) * 0.125).astype(BF16)
        rim_one[1, :, y * 128 : y * 128 + 128] = pooled[0:32]
        rim_one[2, :, y * 128 : y * 128 + 128] = pooled[32:64]

    edge = halo(1, rim_one.at[1], rim_one.at[2], rim_one.at[0], rim_one.at[3])
    for z in (1, 2):
        lay_taps(taps_two, z * 288, rim_one[z], 128)
    edge.wait()
    for z in (0, 3):
        lay_taps(taps_two, z * 288, rim_one[z], 128)
    kernel_two = weight_two[...].reshape(864, 64)
    pairs = [activate(tn(kernel_two, taps_two[z * 288 : z * 288 + 864, :])) for z in range(2)]
    slope_two = [pair[1] for pair in pairs]
    pool = pool_matrix((512, 128), 128)
    rim_two[1] = (mm2(pairs[0][0] + pairs[1][0], pool) * 0.125).astype(BF16)

    edge = halo(2, rim_two.at[1], rim_two.at[1], rim_two.at[0], rim_two.at[2])
    lay_taps(taps_three, 576, rim_two[1], 64)
    finish(cots)
    cot = jnp.concatenate([cot_all[i] for i in range(n)], axis=0).astype(BF16)
    wide = mm(cot, pool_matrix((32, 128), 64, True)) * 0.125
    edge.wait()
    for z in (0, 2):
        lay_taps(taps_three, z * 576, rim_two[z], 64)
    kernel_three = weight_three[...].reshape(1728, 128)
    active, slope = activate(tn(kernel_three, taps_three[0:1728, :]))
    grad = (wide * slope).astype(BF16)
    rim_three[1] = grad

    edge = halo(3, rim_three.at[1], rim_three.at[1], rim_three.at[0], rim_three.at[2])
    lay_taps(wide_three, 1152, grad, 64)
    for part in range(4):
        term = mnt(grad, taps_three[part * 512 : part * 512 + 512, :])
        for i in range(n):
            a_src[part, i] = term[i * share : i * share + share].astype(BF16)
    a_first = [
        pass_to(1, i, beside, a_src.at[2 * i + 1 - core], a_got.at[i]) for i in range(2)
    ]
    paired = mm2(active, pool_matrix((128, 32), 64))
    for i in range(n):
        p_src[i] = paired[i * share : i * share + share]
    p_out[s] = p_src[s]
    feats = spread(2, "space", lambda p: p_src.at[p], p_out.at[s])
    edge.wait()
    finish(a_first)
    for i in range(2):
        a_half[i] = (a_src[2 * i + core].astype(F32) + a_got[i].astype(F32)).astype(BF16)
    a_first = [pass_to(3, 0, across, a_half.at[1 - row], a_other)]
    for z in (0, 2):
        lay_taps(wide_three, z * 1152, rim_three[z], 64)
    flipped = jnp.concatenate([weight_three[26 - t] for t in range(27)], axis=1)
    back = mm(flipped, wide_three[...])
    wide = mm2(back, pool_matrix((128, 512), 128, True)) * 0.125
    grads = [(wide * slope_two[z]).astype(BF16) for z in range(2)]
    for z in range(2):
        rim_four[z + 1] = grads[z]

    edge = halo(4, rim_four.at[1], rim_four.at[2], rim_four.at[0], rim_four.at[3])
    total = mnt(grads[0], taps_two[0:896, :]) + mnt(grads[1], taps_two[288:1184, :])
    stack = jnp.concatenate([total[:, k * 128 : k * 128 + 128] for k in range(7)], axis=0)
    b_src[...] = stack.astype(BF16)
    b_first = [pass_to(5, 0, beside, b_src, b_got)]
    for z in (1, 2):
        lay_taps(wide_two, z * 576, rim_four[z], 128)
    finish(a_first)
    a_sum[...] = (a_half[row].astype(F32) + a_other[...].astype(F32)).astype(BF16)
    a_next[s] = a_sum[s]
    a_second = spread(4, "space", lambda p: a_sum.at[p], a_next.at[s])
    edge.wait()
    finish(b_first)
    b_half[...] = (b_src[...].astype(F32) + b_got[...].astype(F32)).astype(BF16)
    b_first = [pass_to(6, 0, across, b_half, b_other)]
    for z in (0, 3):
        lay_taps(wide_two, z * 576, rim_four[z], 128)
    backs = [mm(back_two[...], wide_two[z * 576 : z * 576 + 1728, :]) for z in range(2)]
    pool = pool_matrix((128, 256), 256, True)
    for y in range(4):
        wides = [mm2(back[:, y * 128 : y * 128 + 128], pool) * 0.125 for back in backs]
        wide = jnp.concatenate([wides[0], wides[0], wides[1], wides[1]], axis=0)
        for part in range(2):
            at = y * 512 + part * 256
            grad_one[:, at : at + 256] = (wide * slope_one[:, at : at + 256]).astype(BF16)
    total = mnt(grad_one[...], taps_one[...])
    c_src[...] = sum(
        mm2(total[32 * z : 32 * z + 32], select[z * 256 : z * 256 + 256, :]) for z in range(4)
    )
    c_slot[d] = c_src[...]
    c_first = spread(7, "dp", lambda p: c_src, c_slot.at[d])

    finish(b_first)
    total = b_half[...].astype(F32) + b_other[...].astype(F32)
    rows = b_sum.shape[1]
    for i in range(n):
        piece = total[i * rows : i * rows + rows]
        if piece.shape[0] < rows:
            piece = jnp.zeros((rows, 128), F32)
        b_sum[i] = piece.astype(BF16)
    b_next[s] = b_sum[s]
    b_second = spread(8, "space", lambda p: b_sum.at[p], b_next.at[s])
    finish(c_first)
    c_sum[...] = added(c_slot, nd)
    c_next[s] = c_sum[...]
    c_second = spread(9, "space", lambda p: c_sum, c_next.at[s])
    finish(a_second)
    a_out[d] = added(a_next, n)
    a_third = spread(10, "dp", lambda p: a_out.at[d], a_out.at[d])
    finish(b_second)
    b_out[s] = added(b_next, n).astype(BF16)
    b_third = spread(11, "space", lambda p: b_out.at[s], b_out.at[s])
    finish(c_second)
    c_out[...] = added(c_next, n)
    for copies in (feats, a_third, b_third):
        finish(copies)


def select_taps():
    table = np.zeros((4, 9, 24, 27, 4), np.float32)
    for z in range(4):
        for spot in range(24):
            if spot < 16:
                channel, plane = spot // 4, spot % 4 + 1
            else:
                channel, plane = spot % 4, 0 if spot < 20 else 5
            if 0 <= plane - z < 3:
                for k in range(9):
                    table[z, k, spot, (plane - z) * 9 + k, channel] = 1.0
    table = np.pad(table.reshape(4, 216, 108), ((0, 0), (0, 40), (0, 20)))
    return jnp.asarray(table.reshape(1024, 128), BF16)


def body(nd, n, volume, first_weight, second_weight, third_weight, feature_cotangent):
    share = feature_cotangent.shape[1]
    depth = feature_cotangent.shape[2]
    weight_one = jnp.pad(first_weight.reshape(108, 32).T, ((0, 0), (0, 20)))
    b_rows = pl.cdiv(448, n)
    most = max(nd, n)
    scratch = [
        ((2, 4, 8, 256), BF16), ((4, 32, 512), BF16), ((3, 64, 128), BF16), ((3, 128, 128), BF16),
        ((4, 64, 512), BF16), ((n, share, 32), F32),
        ((256, 2048), BF16), ((1184, 512), BF16), ((2048, 128), BF16), ((3456, 128), BF16),
        ((2304, 512), BF16), ((128, 2048), F32), ((128, 2048), BF16), ((32, 1728), BF16),
        ((n, share, 32), F32), ((nd, n, share, 512), BF16), ((2, n, share, 512), BF16),
        ((2, n, share, 512), BF16), ((n, share, 512), BF16), ((n, share, 512), BF16),
        ((n, share, 512), BF16),
        ((448, 128), BF16), ((448, 128), BF16), ((448, 128), BF16), ((448, 128), BF16),
        ((n, b_rows, 128), BF16), ((n, b_rows, 128), BF16),
        ((32, 128), F32), ((nd, 32, 128), F32), ((32, 128), F32), ((n, 32, 128), F32),
        ((depth, share, 32), F32), ((16, 8, 256), F32), ((8, 8, 256), F32),
    ]
    third, rest, first, turned = pl.pallas_call(
        functools.partial(step_kernel, nd, n, share),
        out_shape=[
            jax.ShapeDtypeStruct((nd, share, 512), F32),
            jax.ShapeDtypeStruct((n, b_rows, 128), BF16),
            jax.ShapeDtypeStruct((32, 128), F32),
            jax.ShapeDtypeStruct((n, share, 32), F32),
        ],
        in_specs=[VM] * 6,
        out_specs=[VM] * 4,
        scratch_shapes=[pltpu.VMEM(shape, kind) for shape, kind in scratch]
        + [pltpu.SemaphoreType.DMA((5, 2))] * 2
        + [pltpu.SemaphoreType.DMA((12, most))] * 2,
        compiler_params=pltpu.CompilerParams(
            collective_id=1, has_side_effects=True, vmem_limit_bytes=56 << 20
        ),
    )(volume[0], weight_one, select_taps(), second_weight, third_weight, feature_cotangent[0])

    features = turned.reshape(depth, 2, share, 32).sum(axis=1) * 0.125
    features = features.transpose(1, 0, 2).astype(BF16)[None]
    third = third.transpose(1, 0, 2).reshape(share, 2048)[:, :1728]
    third_grad = third.reshape(share, 27, 64).transpose(1, 2, 0)
    rest = rest.reshape(n * b_rows, 128)[:448]
    second = rest.reshape(7, 64, 128).transpose(1, 0, 2).reshape(64, 896)[:, :864]
    second_grad = second.T.reshape(27, 32, 64).astype(F32)
    first_grad = first[:, :108].T.reshape(27, 4, 32)
    return (features, first_grad, second_grad, third_grad)


def solution(mesh):
    return jax.shard_map(
        functools.partial(body, mesh.shape["dp"], mesh.shape["space"]),
        mesh=mesh,
        in_specs=(P("dp", None, "space", None, None), P(), P(), P(), P("dp", "space", None, None)),
        out_specs=(P("dp", "space", None, None), P(), P(), P(None, None, "space")),
        check_vma=False,
    )
```

```python
import functools

import jax
import jax.numpy as jnp
import numpy as np
from jax import lax
from jax.experimental import pallas as pl
from jax.experimental.pallas import tpu as pltpu
from jax.sharding import PartitionSpec as P

MESH = pl.DeviceIdType.MESH
F32 = jnp.float32
BF16 = jnp.bfloat16
VM = pl.BlockSpec(memory_space=pltpu.VMEM)
nt = (((1,), (1,)), ((), ()))


def mm(a, b):
    return jnp.dot(a, b, preferred_element_type=F32)


def halves(v):
    hi = v.astype(BF16)
    return hi, (v - hi.astype(F32)).astype(BF16)


def mm2(v, b):
    hi, lo = halves(v)
    return mm(hi, b) + mm(lo, b)


def activate(v):
    e = jnp.exp(-jnp.abs(v))
    d = 1.0 + e
    leaky = 0.3 * v + 0.7 * (jnp.maximum(v, 0.0) + jnp.log1p(e))
    slope = 0.3 + 0.7 * (jnp.where(v >= 0.0, 1.0, e) / d)
    return leaky, slope


def shifts(x, width):
    length = x.shape[1]
    lane = lax.broadcasted_iota(jnp.int32, x.shape, 1)
    column = lane % width
    zero = jnp.zeros_like(x)
    sides = (
        jnp.where(column >= 1, pltpu.roll(x, 1, 1), zero),
        x,
        jnp.where(column < width - 1, pltpu.roll(x, length - 1, 1), zero),
    )
    taps = []
    for dy in range(3):
        for side in sides:
            if dy == 0:
                tap = jnp.where(lane >= width, pltpu.roll(side, width, 1), zero)
            elif dy == 1:
                tap = side
            else:
                tap = jnp.where(
                    lane < length - width, pltpu.roll(side, length - width, 1), zero
                )
            taps.append(tap)
    return taps


def pool_matrix(shape, width, flip=False):
    a = lax.broadcasted_iota(jnp.int32, shape, 1 if flip else 0)
    b = lax.broadcasted_iota(jnp.int32, shape, 0 if flip else 1)
    row = a // (2 * width)
    return (row * (width // 2) + (a % width) // 2 == b).astype(F32).astype(BF16)


def tn(a, b):
    return lax.dot_general(a, b, (((0,), (0,)), ((), ())), preferred_element_type=F32)


def mnt(a, b):
    return lax.dot_general(a, b, nt, preferred_element_type=F32)


def greet(axes):
    barrier = pltpu.get_barrier_semaphore()
    count = 0
    for axis, n in axes:
        me = lax.axis_index(axis)
        for k in range(1, n):
            pl.semaphore_signal(
                barrier, inc=1, device_id={axis: lax.rem(me + k, n)}, device_id_type=MESH
            )
            count += 1
    pl.semaphore_wait(barrier, count)


def spread_to(axis, n, send, recv, source, target):
    me = lax.axis_index(axis)
    copies = []
    for k in range(1, n):
        peer = lax.rem(me + k, n)
        copy = pltpu.make_async_remote_copy(
            src_ref=source(peer),
            dst_ref=target,
            send_sem=send.at[k],
            recv_sem=recv.at[k],
            device_id={axis: peer},
            device_id_type=MESH,
        )
        copy.start()
        copies.append(copy)
    return copies


def finish(copies):
    for copy in copies:
        copy.wait()


def added(slots, count):
    total = slots[0].astype(F32)
    for k in range(1, count):
        total = total + slots[k].astype(F32)
    return total


class Halo:
    def __init__(self, n, send, recv, first, last, low, high):
        s = lax.axis_index("space")
        self.has_low, self.has_high = s > 0, s < n - 1
        self.up = pltpu.make_async_remote_copy(
            src_ref=last, dst_ref=low, send_sem=send.at[0], recv_sem=recv.at[0],
            device_id={"space": lax.rem(s + 1, n)}, device_id_type=MESH,
        )
        self.down = pltpu.make_async_remote_copy(
            src_ref=first, dst_ref=high, send_sem=send.at[1], recv_sem=recv.at[1],
            device_id={"space": lax.rem(s + n - 1, n)}, device_id_type=MESH,
        )

        @pl.when(self.has_high)
        def _():
            self.up.start()

        @pl.when(self.has_low)
        def _():
            self.down.start()

        @pl.when(s == 0)
        def _():
            low[...] = jnp.zeros_like(low)

        @pl.when(s == n - 1)
        def _():
            high[...] = jnp.zeros_like(high)

    def wait(self):
        @pl.when(self.has_high)
        def _():
            self.down.wait_recv()

        @pl.when(self.has_low)
        def _():
            self.up.wait_recv()

        @pl.when(self.has_high)
        def _():
            self.up.wait_send()

        @pl.when(self.has_low)
        def _():
            self.down.wait_send()


def lay_taps(into, at, block, width):
    taps = jnp.concatenate(shifts(block.astype(F32), width), axis=0).astype(BF16)
    into[at : at + taps.shape[0], :] = taps


def step_kernel(
    nd, n, share, volume, weight_one, select, weight_two, weight_three, cotangent,
    a_out, b_out, c_out, p_out,
    rim_zero, rim_one, rim_two, rim_three, rim_four, cot_all,
    taps_one, taps_two, taps_three, wide_three, wide_two, slope_one, grad_one, back_two,
    p_src, a_src, a_got, a_half, a_other, a_sum, a_next, b_src, b_got, b_half, b_other, b_sum, b_next,
    c_src, c_slot, c_sum, c_next, halo_send, halo_recv, sends, recvs,
):
    d = lax.axis_index("dp")
    s = lax.axis_index("space")
    greet((("dp", nd), ("space", n)))

    def halo(index, first, last, low, high):
        return Halo(n, halo_send.at[index], halo_recv.at[index], first, last, low, high)

    def spread(index, axis, source, target):
        return spread_to(
            axis, nd if axis == "dp" else n, sends.at[index], recvs.at[index], source, target
        )

    core = lax.rem(d, 2)
    row = lax.div(d, 2)
    beside = d + 1 - 2 * core
    across = lax.rem(d + 2, 4)

    def pass_to(index, slot, peer, source, target):
        copy = pltpu.make_async_remote_copy(
            src_ref=source, dst_ref=target, send_sem=sends.at[index, slot],
            recv_sem=recvs.at[index, slot], device_id={"dp": peer}, device_id_type=MESH,
        )
        copy.start()
        return copy

    edge = halo(0, volume.at[0], volume.at[3], rim_zero.at[0], rim_zero.at[1])
    cot_all[s] = cotangent[lax.div(s, 2)]
    cots = spread(0, "space", lambda p: cotangent.at[lax.div(p, 2)], cot_all.at[s])
    for t in range(27):
        back_two[:, t * 64 : t * 64 + 64] = weight_two[26 - t]
    taps_two[1152:1184, :] = jnp.zeros((32, 512), BF16)
    taps_three[1728:2048, :] = jnp.zeros((320, 128), BF16)
    band = jnp.concatenate(
        [mnt(weight_one[...], select[z * 256 : z * 256 + 256, :]) for z in range(4)], axis=0
    ).astype(BF16)
    edge.wait()

    planes = [rim_zero[0]] + [volume[z] for z in range(4)] + [rim_zero[1]]
    planes = jnp.concatenate([plane.astype(F32) for plane in planes], axis=0)
    taps = shifts(planes, 256)
    taps = jnp.concatenate(taps + [jnp.zeros((40, 2048), F32)], axis=0)
    taps_one[...] = taps.astype(BF16)
    active, slope = activate(mm(band, taps_one[...]))
    slope_one[...] = slope
    deep = jnp.concatenate(
        [active[0:32] + active[32:64], active[64:96] + active[96:128]], axis=0
    )
    pool = pool_matrix((256, 128), 256)
    for y in range(4):
        low = deep[:, y * 512 : y * 512 + 256]
        high = deep[:, y * 512 + 256 : y * 512 + 512]
        pooled = (mm2(low + high, pool) * 0.125).astype(BF16)
        rim_one[1, :, y * 128 : y * 128 + 128] = pooled[0:32]
        rim_one[2, :, y * 128 : y * 128 + 128] = pooled[32:64]

    edge = halo(1, rim_one.at[1], rim_one.at[2], rim_one.at[0], rim_one.at[3])
    for z in (1, 2):
        lay_taps(taps_two, z * 288, rim_one[z], 128)
    edge.wait()
    for z in (0, 3):
        lay_taps(taps_two, z * 288, rim_one[z], 128)
    kernel_two = weight_two[...].reshape(864, 64)
    pairs = [activate(tn(kernel_two, taps_two[z * 288 : z * 288 + 864, :])) for z in range(2)]
    slope_two = [pair[1] for pair in pairs]
    pool = pool_matrix((512, 128), 128)
    rim_two[1] = (mm2(pairs[0][0] + pairs[1][0], pool) * 0.125).astype(BF16)

    edge = halo(2, rim_two.at[1], rim_two.at[1], rim_two.at[0], rim_two.at[2])
    lay_taps(taps_three, 576, rim_two[1], 64)
    finish(cots)
    cot = jnp.concatenate([cot_all[i] for i in range(n)], axis=0).astype(BF16)
    wide = mm(cot, pool_matrix((32, 128), 64, True)) * 0.125
    edge.wait()
    for z in (0, 2):
        lay_taps(taps_three, z * 576, rim_two[z], 64)
    kernel_three = weight_three[...].reshape(1728, 128)
    active, slope = activate(tn(kernel_three, taps_three[0:1728, :]))
    grad = (wide * slope).astype(BF16)
    rim_three[1] = grad

    edge = halo(3, rim_three.at[1], rim_three.at[1], rim_three.at[0], rim_three.at[2])
    lay_taps(wide_three, 1152, grad, 64)
    for part in range(4):
        term = mnt(grad, taps_three[part * 512 : part * 512 + 512, :])
        for i in range(n):
            a_src[part, i] = term[i * share : i * share + share].astype(BF16)
    a_first = [
        pass_to(1, i, beside, a_src.at[2 * i + 1 - core], a_got.at[i]) for i in range(2)
    ]
    paired = mm2(active, pool_matrix((128, 32), 64))
    for i in range(n):
        p_src[i] = paired[i * share : i * share + share]
    p_out[s] = p_src[s]
    feats = spread(2, "space", lambda p: p_src.at[p], p_out.at[s])
    edge.wait()
    finish(a_first)
    for i in range(2):
        a_half[i] = (a_src[2 * i + core].astype(F32) + a_got[i].astype(F32)).astype(BF16)
    a_first = [pass_to(3, 0, across, a_half.at[1 - row], a_other)]
    for z in (0, 2):
        lay_taps(wide_three, z * 1152, rim_three[z], 64)
    flipped = jnp.concatenate([weight_three[26 - t] for t in range(27)], axis=1)
    back = mm(flipped, wide_three[...])
    wide = mm2(back, pool_matrix((128, 512), 128, True)) * 0.125
    grads = [(wide * slope_two[z]).astype(BF16) for z in range(2)]
    for z in range(2):
        rim_four[z + 1] = grads[z]

    edge = halo(4, rim_four.at[1], rim_four.at[2], rim_four.at[0], rim_four.at[3])
    total = mnt(grads[0], taps_two[0:896, :]) + mnt(grads[1], taps_two[288:1184, :])
    stack = jnp.concatenate([total[:, k * 128 : k * 128 + 128] for k in range(7)], axis=0)
    b_src[...] = stack.astype(BF16)
    b_first = [pass_to(5, 0, beside, b_src, b_got)]
    for z in (1, 2):
        lay_taps(wide_two, z * 576, rim_four[z], 128)
    finish(a_first)
    a_sum[...] = (a_half[row].astype(F32) + a_other[...].astype(F32)).astype(BF16)
    a_next[s] = a_sum[s]
    a_second = spread(4, "space", lambda p: a_sum.at[p], a_next.at[s])
    edge.wait()
    finish(b_first)
    b_half[...] = (b_src[...].astype(F32) + b_got[...].astype(F32)).astype(BF16)
    b_first = [pass_to(6, 0, across, b_half, b_other)]
    for z in (0, 3):
        lay_taps(wide_two, z * 576, rim_four[z], 128)
    backs = [mm(back_two[...], wide_two[z * 576 : z * 576 + 1728, :]) for z in range(2)]
    pool = pool_matrix((128, 256), 256, True)
    for y in range(4):
        wides = [mm2(back[:, y * 128 : y * 128 + 128], pool) * 0.125 for back in backs]
        wide = jnp.concatenate([wides[0], wides[0], wides[1], wides[1]], axis=0)
        for part in range(2):
            at = y * 512 + part * 256
            grad_one[:, at : at + 256] = (wide * slope_one[:, at : at + 256]).astype(BF16)
    total = mnt(grad_one[...], taps_one[...])
    c_src[...] = sum(
        mm2(total[32 * z : 32 * z + 32], select[z * 256 : z * 256 + 256, :]) for z in range(4)
    )
    c_slot[d] = c_src[...]
    c_first = spread(7, "dp", lambda p: c_src, c_slot.at[d])

    finish(b_first)
    total = b_half[...].astype(F32) + b_other[...].astype(F32)
    rows = b_sum.shape[1]
    for i in range(n):
        piece = total[i * rows : i * rows + rows]
        if piece.shape[0] < rows:
            piece = jnp.zeros((rows, 128), F32)
        b_sum[i] = piece.astype(BF16)
    b_next[s] = b_sum[s]
    b_second = spread(8, "space", lambda p: b_sum.at[p], b_next.at[s])
    finish(c_first)
    c_sum[...] = added(c_slot, nd)
    c_next[s] = c_sum[...]
    c_second = spread(9, "space", lambda p: c_sum, c_next.at[s])
    finish(a_second)
    a_out[d] = added(a_next, n)
    a_third = spread(10, "dp", lambda p: a_out.at[d], a_out.at[d])
    finish(b_second)
    b_out[s] = added(b_next, n).astype(BF16)
    b_third = spread(11, "space", lambda p: b_out.at[s], b_out.at[s])
    finish(c_second)
    c_out[...] = added(c_next, n)
    for copies in (feats, a_third, b_third):
        finish(copies)


def select_taps():
    table = np.zeros((4, 9, 24, 27, 4), np.float32)
    for z in range(4):
        for spot in range(24):
            channel, plane = spot % 4, spot // 4
            if 0 <= plane - z < 3:
                for k in range(9):
                    table[z, k, spot, (plane - z) * 9 + k, channel] = 1.0
    table = np.pad(table.reshape(4, 216, 108), ((0, 0), (0, 40), (0, 20)))
    return jnp.asarray(table.reshape(1024, 128), BF16)


def body(nd, n, volume, first_weight, second_weight, third_weight, feature_cotangent):
    share = feature_cotangent.shape[1]
    depth = feature_cotangent.shape[2]
    weight_one = jnp.pad(first_weight.reshape(108, 32).T, ((0, 0), (0, 20)))
    planes = volume[0].transpose(1, 0, 2, 3).reshape(4, 4, 2048)
    cotangent = feature_cotangent[0].transpose(1, 0, 2).astype(F32)
    b_rows = pl.cdiv(448, n)
    most = max(nd, n)
    scratch = [
        ((2, 4, 2048), BF16), ((4, 32, 512), BF16), ((3, 64, 128), BF16), ((3, 128, 128), BF16),
        ((4, 64, 512), BF16), ((n, share, 32), F32),
        ((256, 2048), BF16), ((1184, 512), BF16), ((2048, 128), BF16), ((3456, 128), BF16),
        ((2304, 512), BF16), ((128, 2048), F32), ((128, 2048), BF16), ((32, 1728), BF16),
        ((n, share, 32), F32), ((nd, n, share, 512), BF16), ((2, n, share, 512), BF16),
        ((2, n, share, 512), BF16), ((n, share, 512), BF16), ((n, share, 512), BF16),
        ((n, share, 512), BF16),
        ((448, 128), BF16), ((448, 128), BF16), ((448, 128), BF16), ((448, 128), BF16),
        ((n, b_rows, 128), BF16), ((n, b_rows, 128), BF16),
        ((32, 128), F32), ((nd, 32, 128), F32), ((32, 128), F32), ((n, 32, 128), F32),
    ]
    third, rest, first, turned = pl.pallas_call(
        functools.partial(step_kernel, nd, n, share),
        out_shape=[
            jax.ShapeDtypeStruct((nd, share, 512), F32),
            jax.ShapeDtypeStruct((n, b_rows, 128), BF16),
            jax.ShapeDtypeStruct((32, 128), F32),
            jax.ShapeDtypeStruct((n, share, 32), F32),
        ],
        in_specs=[VM] * 6,
        out_specs=[VM] * 4,
        scratch_shapes=[pltpu.VMEM(shape, kind) for shape, kind in scratch]
        + [pltpu.SemaphoreType.DMA((5, 2))] * 2
        + [pltpu.SemaphoreType.DMA((12, most))] * 2,
        compiler_params=pltpu.CompilerParams(
            collective_id=1, has_side_effects=True, vmem_limit_bytes=56 << 20
        ),
    )(planes, weight_one, select_taps(), second_weight, third_weight, cotangent)

    features = turned.reshape(depth, 2, share, 32).sum(axis=1) * 0.125
    features = features.transpose(1, 0, 2).astype(BF16)[None]
    third = third.transpose(1, 0, 2).reshape(share, 2048)[:, :1728]
    third_grad = third.reshape(share, 27, 64).transpose(1, 2, 0)
    rest = rest.reshape(n * b_rows, 128)[:448]
    second = rest.reshape(7, 64, 128).transpose(1, 0, 2).reshape(64, 896)[:, :864]
    second_grad = second.T.reshape(27, 32, 64).astype(F32)
    first_grad = first[:, :108].T.reshape(27, 4, 32)
    return (features, first_grad, second_grad, third_grad)


def solution(mesh):
    return jax.shard_map(
        functools.partial(body, mesh.shape["dp"], mesh.shape["space"]),
        mesh=mesh,
        in_specs=(P("dp", None, "space", None, None), P(), P(), P(), P("dp", "space", None, None)),
        out_specs=(P("dp", "space", None, None), P(), P(), P(None, None, "space")),
        check_vma=False,
    )
```
